32 devices in a mesh: row: 8 (over y, x, core), col: 4 (over z).
Axes of the slice: x: 2, y: 2, z: 4, core: 2. Of those that a mesh axis runs over, the one named last changes fastest.
Arguments:
- features: bfloat16 [1024, 4, 512], P('row', 'col'), may hold values from -6 to 6
- adj_blocks: bfloat16 [8, 4, 128, 128, 128], P('row', 'col'), may hold values from -0.0625 to 0.0625
- block_rows: int32 [8, 4, 128], P('row', 'col'), may hold values from 0 to 3
- block_cols: int32 [8, 4, 128], P('row', 'col'), may hold values from 0 to 7
- block_counts: int32 [8, 4], P('row', 'col'), may hold values from 16 to 128, as said below
- w_qkv: bfloat16 [512, 1536], replicated, may hold values from -0.25 to 0.25
Outputs:
- aggregated: bfloat16 [4096, 512], P(('row', 'col'))
- qkv: bfloat16 [4096, 1536], P(('row', 'col'))
The draws below stay inside these ranges and needn't reach their ends.
Inputs may be any that keep to these rules, and one draw needn't show every extreme that they name: `block_counts`: some tile has exactly 128 live slots and some exactly 16.
All inputs are finite; a program needn't handle non-finite values.
Results may differ from the reference program's by a relative error of at most 0.012.
Values may be sent and summed in bfloat16 or wider, within the bound.
A program may use at most 128 MiB of HBM per device.

```python
import jax
import jax.numpy as jnp
from jax import lax

F = 512
BLOCK = 128
CELL_DEV = 128
SLOTS = 128
CELLS = 4096
PANEL = 1024
TILE_ROWS = 512
ROW_BLOCKS = 4
COL_BLOCKS = 8
N_ROW = 8
N_COL = 4


def draw_block_counts(key, part):
    shifts = jax.random.randint(jax.random.fold_in(key, 11), (N_ROW, N_COL), 0, 4)
    counts = jnp.maximum(jnp.right_shift(jnp.full((N_ROW, N_COL), SLOTS, jnp.int32), shifts.astype(jnp.int32)), 1)
    counts = counts.at[0, 0].set(SLOTS)
    counts = counts.at[N_ROW - 1, N_COL - 1].set(SLOTS // 8)
    return counts.astype(jnp.int32)


def place_ends(array, own_key, low, high):
    place = [jax.random.randint(jax.random.fold_in(own_key, axis), (), 0, length) for axis, length in enumerate(array.shape)]
    main_axis = array.shape.index(max(array.shape))
    neighbour = place[:main_axis] + [(place[main_axis] + 1) % array.shape[main_axis]] + place[main_axis + 1:]
    return array.at[tuple(place)].set(low).at[tuple(neighbour)].set(high)


def block_levels(stream_key, shape, split, low, top_value):
    factor_of = 1.0
    for dim, blocks in split:
        heights = jax.random.uniform(jax.random.fold_in(jax.random.fold_in(stream_key, 6), dim), (blocks,), jnp.float32, low / len(split), top_value / len(split))
        factor_of = factor_of * jnp.repeat(jnp.exp(heights), shape[dim] // blocks).reshape((-1,) + (1,) * (len(shape) - 1 - dim))
    return factor_of


def bell_draw(own_key, extent, deviation, bound, shards=(), kind=jnp.bfloat16):
    result = jax.random.normal(own_key, extent, jnp.float32) * deviation
    if len(shards) > 0:
        result = block_levels(own_key, extent, shards, -0.22, 0.18) * result
    return jnp.clip(result, min=-bound, max=bound).astype(kind)


def setup_inputs(seed: int = 0) -> dict:
    key_list = jax.random.split(jax.random.key(seed), 7)
    return {
        "features": bell_draw(key_list[0], (PANEL, N_COL, F), 1.0, 6.0, ((0, 8), (1, 4))),
        "adj_blocks": bell_draw(key_list[1], (N_ROW, N_COL, SLOTS, BLOCK, BLOCK), (BLOCK * BLOCK * SLOTS // (2 * CELL_DEV)) ** -0.5, 0.0625, ((0, 8), (1, 4))),
        "block_rows": place_ends(jax.random.randint(key_list[2], (N_ROW, N_COL, SLOTS), 0, ROW_BLOCKS), jax.random.fold_in(key_list[2], 1), 0, ROW_BLOCKS - 1).astype(jnp.int32),
        "block_cols": place_ends(jax.random.randint(key_list[3], (N_ROW, N_COL, SLOTS), 0, COL_BLOCKS), jax.random.fold_in(key_list[3], 1), 0, COL_BLOCKS - 1).astype(jnp.int32),
        "block_counts": draw_block_counts(jax.random.fold_in(key_list[6], 71), 0),
        "w_qkv": bell_draw(key_list[5], (F, 3 * F), F ** -0.5, 0.25),
    }


def tile_partial(tile_blocks, row_ids, col_ids, live_count, feature_panel):
    start_sum = jnp.zeros((TILE_ROWS, F), jnp.float32)

    def add_slot(slot, partial_value):
        def live_slot(current_sum):
            first_col = (col_ids[slot] * BLOCK).astype(jnp.int32)
            first_row = (row_ids[slot] * BLOCK).astype(jnp.int32)
            block_feats = lax.dynamic_slice_in_dim(feature_panel, first_col, BLOCK, 0)
            product = jnp.dot(tile_blocks[slot], block_feats, preferred_element_type=jnp.float32)
            current = lax.dynamic_slice_in_dim(current_sum, first_row, BLOCK, 0)
            return lax.dynamic_update_slice_in_dim(current_sum, current + product, first_row, 0)

        return lax.cond(slot < live_count, live_slot, lambda keep_sum: keep_sum, partial_value)

    return lax.fori_loop(0, SLOTS, add_slot, start_sum)


def reference(features, adj_blocks, block_rows, block_cols, block_counts, w_qkv):
    def grid_row(row_index):
        def add_tile(col_index, total):
            feature_panel = lax.dynamic_index_in_dim(features, col_index, 1, keepdims=False)
            tile_blocks = adj_blocks[row_index, col_index]
            partial_value = tile_partial(tile_blocks, block_rows[row_index, col_index], block_cols[row_index, col_index], block_counts[row_index, col_index], feature_panel)
            rounded = lax.optimization_barrier(partial_value.astype(jnp.bfloat16))
            return total + rounded.astype(jnp.float32)

        total = lax.fori_loop(0, N_COL, add_tile, jnp.zeros((TILE_ROWS, F), jnp.float32))
        return total.astype(jnp.bfloat16)

    stacked = lax.map(grid_row, jnp.arange(N_ROW, dtype=jnp.int32))
    aggregated = stacked.reshape(CELLS, F)
    qkv = jnp.dot(aggregated, w_qkv, preferred_element_type=jnp.float32).astype(jnp.bfloat16)
    return (aggregated, qkv)
```

```python
import functools

import jax
import jax.numpy as jnp
from jax import lax
from jax.experimental import pallas as pl
from jax.experimental.pallas import tpu as pltpu
from jax.sharding import PartitionSpec as P

MESH = pl.DeviceIdType.MESH
CHUNK = 128
UNROLL = 4


def fused_kernel(
    n_col, feats, adj, rows, cols, count, w, agg, qkv,
    adj_v, prefix, dense, panel, part, got, w_v, meta_v, meta_s,
    local_sem, gather_send, gather_recv, relay_send, sum_send, sum_recv,
):
    slots, side = adj_v.shape[0], adj_v.shape[1]
    n_chunk, n_row = panel.shape[0], panel.shape[1]
    width = panel.shape[3]
    row, col = lax.axis_index("row"), lax.axis_index("col")
    chip_y, chip_x, core = row // 4, (row // 2) % 2, row % 2

    def partner(code):
        y = 1 - chip_y if code & 4 else chip_y
        x = 1 - chip_x if code & 2 else chip_x
        k = 1 - core if code & 1 else core
        return (y * 2 + x) * 2 + k

    adj_copy = pltpu.make_async_copy(adj, adj_v, local_sem.at[0])
    adj_copy.start()
    w_copy = pltpu.make_async_copy(w, w_v, local_sem.at[1])
    w_copy.start()

    barrier = pltpu.get_barrier_semaphore()
    for code in (1, 2, 4, 6):
        pl.semaphore_signal(barrier, inc=1, device_id={"row": partner(code)}, device_id_type=MESH)
    for step in range(1, n_col):
        pl.semaphore_signal(
            barrier, inc=1, device_id={"col": lax.rem(col + step, n_col)}, device_id_type=MESH
        )

    lane = lax.broadcasted_iota(jnp.int32, (slots, slots), 1)
    sub = lax.broadcasted_iota(jnp.int32, (slots, slots), 0)
    coords = (dense.shape[0] // side) * n_row
    key = rows[...] * n_row + cols[...]
    key_lane = jnp.where(lane < count[0, 0], jnp.broadcast_to(key, (slots, slots)), coords)
    key_sub = jnp.transpose(key_lane)
    same_before = jnp.sum(
        ((key_lane == key_sub) & (lane < sub)).astype(jnp.int32), axis=1, keepdims=True
    )
    less = jnp.sum((key_lane < key_sub).astype(jnp.int32), axis=1, keepdims=True)
    placed = (less + same_before) == lane
    order = jnp.sum(jnp.where(placed, sub, 0), axis=0, keepdims=True)
    keep = jnp.sum(
        jnp.where(placed & (same_before > 0), 1, 0), axis=0, keepdims=True
    )
    upto = jnp.sum((key_sub <= lane).astype(jnp.int32), axis=0, keepdims=True)
    here = jnp.sum((key_sub == lane).astype(jnp.int32), axis=0, keepdims=True)
    last = jnp.where(here > 0, upto - 1, slots)
    meta_v[0:1, :] = order
    meta_v[1:2, :] = keep
    meta_v[2:3, :] = last
    meta_v[3:8, :] = jnp.zeros((5, slots), jnp.int32)
    meta_copy = pltpu.make_async_copy(meta_v, meta_s, local_sem.at[2])
    meta_copy.start()

    panel_own = [feats.at[:, pl.ds(ch * width, width)] for ch in range(n_chunk)]
    pl.semaphore_wait(barrier, 4 + n_col - 1)

    sends = []
    for ch in range(n_chunk):
        for slot, code in enumerate((6, 2, 4, 1)):
            copy = pltpu.make_async_remote_copy(
                src_ref=panel_own[ch],
                dst_ref=panel.at[ch, row],
                send_sem=gather_send.at[ch, slot],
                recv_sem=gather_recv.at[ch, code],
                device_id={"row": partner(code)},
                device_id_type=MESH,
            )
            copy.start()
            sends.append(copy)

    for ch in range(n_chunk):
        panel[ch, row] = feats[:, ch * width:(ch + 1) * width]
    prefix[slots] = jnp.zeros((side, side), prefix.dtype)
    meta_copy.wait()
    adj_copy.wait()

    def add_slots(group, running):
        for inner in range(UNROLL):
            at = group * UNROLL + inner
            held = meta_s[1, at].astype(jnp.float32)
            running = running * held + adj_v[meta_s[0, at]].astype(jnp.float32)
            prefix[at] = running.astype(prefix.dtype)
        return running

    lax.fori_loop(0, slots // UNROLL, add_slots, jnp.zeros((side, side), jnp.float32))
    for block_row in range(dense.shape[0] // side):
        for block_col in range(n_row):
            dense[
                block_row * side:(block_row + 1) * side,
                block_col * side:(block_col + 1) * side,
            ] = prefix[meta_s[2, block_row * n_row + block_col]]

    def arrival(ch, code):
        return pltpu.make_async_remote_copy(
            src_ref=panel_own[ch],
            dst_ref=panel.at[ch, partner(code)],
            send_sem=gather_send.at[ch, 0],
            recv_sem=gather_recv.at[ch, code],
            device_id={"row": partner(1)},
            device_id_type=MESH,
        )

    def relay(ch):
        for slot, code in enumerate((2, 4, 6)):
            arrival(ch, code).wait_recv()
            copy = pltpu.make_async_remote_copy(
                src_ref=panel.at[ch, partner(code)],
                dst_ref=panel.at[ch, partner(code)],
                send_sem=relay_send.at[ch, slot],
                recv_sem=gather_recv.at[ch, code + 1],
                device_id={"row": partner(1)},
                device_id_type=MESH,
            )
            copy.start()
            sends.append(copy)

    summed = []
    relay(0)
    for ch in range(n_chunk):
        if ch + 1 < n_chunk:
            relay(ch + 1)
        for code in (1, 3, 5, 7):
            arrival(ch, code).wait_recv()
        product = jnp.dot(
            dense[...],
            panel[ch].reshape(n_row * side, width),
            preferred_element_type=jnp.float32,
        )
        part[ch] = product.reshape(n_col, side, width).astype(part.dtype)
        now = []
        for step in range(n_col - 1, 0, -1):
            to = lax.rem(col + step, n_col)
            copy = pltpu.make_async_remote_copy(
                src_ref=part.at[ch, to],
                dst_ref=got.at[ch, step - 1],
                send_sem=sum_send.at[ch, step - 1],
                recv_sem=sum_recv.at[ch, step - 1],
                device_id={"col": to},
                device_id_type=MESH,
            )
            copy.start()
            now.append(copy)
        summed.append(now)

    w_copy.wait()
    for ch in range(n_chunk):
        total = part[ch, col].astype(jnp.float32)
        for copy in summed[ch]:
            copy.wait_recv()
        for step in range(n_col - 1):
            total = total + got[ch, step].astype(jnp.float32)
        agg[:, ch * width:(ch + 1) * width] = total.astype(agg.dtype)
    qkv[...] = jnp.dot(agg[...], w_v[...], preferred_element_type=jnp.float32).astype(qkv.dtype)
    for now in summed:
        for copy in now:
            copy.wait_send()
    for copy in sends:
        copy.wait_send()


def fused_body(n_row, n_col, features, adj_blocks, block_rows, block_cols, block_counts, w_qkv):
    cells, feat_width = features.shape[0], features.shape[2]
    slots, side = adj_blocks.shape[2], adj_blocks.shape[3]
    out_width = w_qkv.shape[1]
    n_chunk = feat_width // CHUNK
    vmem = pl.BlockSpec(memory_space=pltpu.VMEM)
    hbm = pl.BlockSpec(memory_space=pl.ANY)
    dma = pltpu.SemaphoreType.DMA
    kind = features.dtype
    return pl.pallas_call(
        functools.partial(fused_kernel, n_col),
        out_shape=(
            jax.ShapeDtypeStruct((cells, feat_width), kind),
            jax.ShapeDtypeStruct((cells, out_width), kind),
        ),
        in_specs=[vmem, hbm, vmem, vmem, pl.BlockSpec(memory_space=pltpu.SMEM), hbm],
        out_specs=(vmem, vmem),
        scratch_shapes=[
            pltpu.VMEM((slots, side, side), kind),
            pltpu.VMEM((slots + 1, side, side), kind),
            pltpu.VMEM((n_col * side, n_row * side), kind),
            pltpu.VMEM((n_chunk, n_row, side, CHUNK), kind),
            pltpu.VMEM((n_chunk, n_col, side, CHUNK), kind),
            pltpu.VMEM((n_chunk, n_col - 1, side, CHUNK), kind),
            pltpu.VMEM(w_qkv.shape, kind),
            pltpu.VMEM((8, slots), jnp.int32),
            pltpu.SMEM((8, slots), jnp.int32),
            dma((3,)),
            dma((n_chunk, 4)),
            dma((n_chunk, 8)),
            dma((n_chunk, 3)),
            dma((n_chunk, n_col - 1)),
            dma((n_chunk, n_col - 1)),
        ],
        compiler_params=pltpu.CompilerParams(
            collective_id=0, has_side_effects=True, vmem_limit_bytes=48 << 20
        ),
    )(
        features[:, 0, :], adj_blocks[0, 0], block_rows[0], block_cols[0], block_counts, w_qkv
    )


def general_body(features, adj_blocks, block_rows, block_cols, block_counts, w_qkv):
    tile_blocks, row_ids, col_ids = adj_blocks[0, 0], block_rows[0, 0], block_cols[0, 0]
    side, feat_width = tile_blocks.shape[1], features.shape[2]
    slots = tile_blocks.shape[0]
    group = 32
    tile_cells = features.shape[0] * lax.axis_size("col")
    live = jnp.arange(slots, dtype=jnp.int32) < block_counts[0, 0]
    gathered = lax.all_gather(features, "row", axis=0, tiled=True)
    panel = gathered[:, 0, :].reshape(-1, side, feat_width)

    def one_group(partial_value, inputs):
        blocks_now, rows_now, cols_now, live_now = inputs
        products = jnp.einsum(
            "gij,gjf->gif", blocks_now, jnp.take(panel, cols_now, axis=0),
            preferred_element_type=jnp.float32,
        )
        products = jnp.where(live_now[:, None, None], products, jnp.float32(0.0))
        return partial_value.at[rows_now].add(products), None

    start = jnp.zeros((tile_cells // side, side, feat_width), jnp.float32)
    partial_value, _ = lax.scan(
        one_group, start,
        (
            tile_blocks.reshape(-1, group, side, side),
            row_ids.reshape(-1, group), col_ids.reshape(-1, group), live.reshape(-1, group),
        ),
    )
    summed = lax.psum_scatter(
        partial_value.reshape(tile_cells, feat_width).astype(jnp.bfloat16),
        "col", scatter_dimension=0, tiled=True,
    )
    qkv = jnp.dot(summed, w_qkv, preferred_element_type=jnp.float32).astype(jnp.bfloat16)
    return summed, qkv


def solution(mesh):
    n_row, n_col = mesh.shape["row"], mesh.shape["col"]
    body = functools.partial(fused_body, n_row, n_col) if n_row == 8 and n_col <= 8 else general_body
    placed = (
        P("row", "col", None),
        P("row", "col", None, None, None),
        P("row", "col", None),
        P("row", "col", None),
        P("row", "col"),
        P(),
    )
    return jax.shard_map(
        body,
        mesh=mesh,
        in_specs=placed,
        out_specs=(P(("row", "col"), None), P(("row", "col"), None)),
        check_vma=False,
    )
```

```python
import functools

import jax
import jax.numpy as jnp
from jax import lax
from jax.experimental import pallas as pl
from jax.experimental.pallas import tpu as pltpu
from jax.sharding import PartitionSpec as P

MESH = pl.DeviceIdType.MESH
CHUNK = 128
UNROLL = 4
AHEAD = 4


def fused_kernel(
    n_col, feats, adj, rows, cols, count, w, agg, qkv,
    adj_v, prefix, dense, panel, part, got, joint, rough, w_v, coords_v, meta_v, meta_s,
    local_sem, gather_send, gather_recv, relay_send, sum_send, sum_recv,
):
    slots, side = adj_v.shape[0], adj_v.shape[1]
    n_chunk, n_row = panel.shape[0], panel.shape[1]
    width = panel.shape[3]
    row, col = lax.axis_index("row"), lax.axis_index("col")
    chip_y, chip_x, core = row // 4, (row // 2) % 2, row % 2

    def partner(code):
        y = 1 - chip_y if code & 4 else chip_y
        x = 1 - chip_x if code & 2 else chip_x
        k = 1 - core if code & 1 else core
        return (y * 2 + x) * 2 + k

    coords_copies = [
        pltpu.make_async_copy(rows, coords_v.at[0:1], local_sem.at[3]),
        pltpu.make_async_copy(cols, coords_v.at[8:9], local_sem.at[4]),
    ]
    for copy in coords_copies:
        copy.start()
    adj_copy = pltpu.make_async_copy(adj, adj_v, local_sem.at[0])
    adj_copy.start()
    panel_own = [feats.at[:, pl.ds(ch * width, width)] for ch in range(n_chunk)]
    own_copies = [
        pltpu.make_async_copy(panel_own[ch], panel.at[ch, row], local_sem.at[5 + ch])
        for ch in range(n_chunk)
    ]
    for copy in own_copies:
        copy.start()
    w_copy = pltpu.make_async_copy(w, w_v, local_sem.at[1])
    w_copy.start()

    barrier = pltpu.get_barrier_semaphore()
    for code in (1, 2, 4, 6):
        pl.semaphore_signal(barrier, inc=1, device_id={"row": partner(code)}, device_id_type=MESH)
    for step in range(1, n_col):
        pl.semaphore_signal(
            barrier, inc=1, device_id={"col": lax.rem(col + step, n_col)}, device_id_type=MESH
        )

    lane = lax.broadcasted_iota(jnp.int32, (slots, slots), 1)
    sub = lax.broadcasted_iota(jnp.int32, (slots, slots), 0)
    coords = (dense.shape[0] // side) * n_row
    for copy in coords_copies:
        copy.wait()
    key = coords_v[0:1, :] * n_row + coords_v[8:9, :]
    key_lane = jnp.where(lane < count[0, 0], jnp.broadcast_to(key, (slots, slots)), coords)
    key_sub = jnp.transpose(key_lane)
    same_before = jnp.sum(
        ((key_lane == key_sub) & (lane < sub)).astype(jnp.int32), axis=1, keepdims=True
    )
    less = jnp.sum((key_lane < key_sub).astype(jnp.int32), axis=1, keepdims=True)
    placed = (less + same_before) == lane
    order = jnp.sum(jnp.where(placed, sub, 0), axis=0, keepdims=True)
    keep = jnp.sum(
        jnp.where(placed & (same_before > 0), 1, 0), axis=0, keepdims=True
    )
    upto = jnp.sum((key_sub <= lane).astype(jnp.int32), axis=0, keepdims=True)
    here = jnp.sum((key_sub == lane).astype(jnp.int32), axis=0, keepdims=True)
    last = jnp.where(here > 0, upto - 1, slots)
    meta_v[0:1, :] = order
    meta_v[1:2, :] = keep
    meta_v[2:3, :] = last
    meta_v[3:8, :] = jnp.zeros((5, slots), jnp.int32)
    meta_copy = pltpu.make_async_copy(meta_v, meta_s, local_sem.at[2])
    meta_copy.start()

    pl.semaphore_wait(barrier, 4 + n_col - 1)

    sends = []

    def send_own(ch):
        for slot, code in enumerate((6, 2, 4, 1)):
            copy = pltpu.make_async_remote_copy(
                src_ref=panel_own[ch],
                dst_ref=panel.at[ch, row],
                send_sem=gather_send.at[ch, slot],
                recv_sem=gather_recv.at[ch, code],
                device_id={"row": partner(code)},
                device_id_type=MESH,
            )
            copy.start()
            sends.append(copy)

    for ch in range(min(AHEAD, n_chunk)):
        send_own(ch)
    prefix[slots] = jnp.zeros((side, side), prefix.dtype)
    meta_copy.wait()
    adj_copy.wait()

    def add_slots(group, running):
        for inner in range(UNROLL):
            at = group * UNROLL + inner
            held = meta_s[1, at].astype(jnp.float32)
            running = running * held + adj_v[meta_s[0, at]].astype(jnp.float32)
            prefix[at] = running.astype(prefix.dtype)
        return running

    lax.fori_loop(0, slots // UNROLL, add_slots, jnp.zeros((side, side), jnp.float32))
    for block_row in range(dense.shape[0] // side):
        for block_col in range(n_row):
            dense[
                block_row * side:(block_row + 1) * side,
                block_col * side:(block_col + 1) * side,
            ] = prefix[meta_s[2, block_row * n_row + block_col]]

    def arrival(ch, code):
        return pltpu.make_async_remote_copy(
            src_ref=panel_own[ch],
            dst_ref=panel.at[ch, partner(code)],
            send_sem=gather_send.at[ch, 0],
            recv_sem=gather_recv.at[ch, code],
            device_id={"row": partner(1)},
            device_id_type=MESH,
        )

    def relay(ch):
        for slot, code in enumerate((2, 4, 6)):
            arrival(ch, code).wait_recv()
            copy = pltpu.make_async_remote_copy(
                src_ref=panel.at[ch, partner(code)],
                dst_ref=panel.at[ch, partner(code)],
                send_sem=relay_send.at[ch, slot],
                recv_sem=gather_recv.at[ch, code + 1],
                device_id={"row": partner(1)},
                device_id_type=MESH,
            )
            copy.start()
            sends.append(copy)

    at_end = (col == 0) | (col == n_col - 1)
    upper = col // 2

    def along(place):
        return place + upper * (n_col - 1 - 2 * place)

    def sum_copy(ch, source, slot, place, sem):
        return pltpu.make_async_remote_copy(
            src_ref=source,
            dst_ref=got.at[ch, slot],
            send_sem=sum_send.at[ch, sem],
            recv_sem=sum_recv.at[ch, slot],
            device_id={"col": along(place)},
            device_id_type=MESH,
        )

    def arrived(ch, slot):
        sum_copy(ch, part.at[ch, 0], slot, 2, 0).wait_recv()

    def send_parts(ch):
        @pl.when(at_end)
        def _():
            sum_copy(ch, part.at[ch, along(3)], 3, 1, 0).start()
            sum_copy(ch, part.at[ch, along(2)], 2, 2, 1).start()
            sum_copy(ch, part.at[ch, along(1)], 0, 1, 2).start()

        @pl.when(jnp.logical_not(at_end))
        def _():
            sum_copy(ch, part.at[ch, along(2)], 1, 2, 1).start()
            sum_copy(ch, part.at[ch, along(0)], 0, 0, 2).start()

    def pass_on(ch):
        @pl.when(jnp.logical_not(at_end))
        def _():
            arrived(ch, 3)
            both = part[ch, along(3)].astype(jnp.float32) + got[ch, 3].astype(jnp.float32)
            joint[ch] = both.astype(joint.dtype)
            sum_copy(ch, joint.at[ch], 1, 3, 0).start()

    def finish(ch):
        lanes = slice(ch * width, (ch + 1) * width)
        for slot in (0, 1):
            arrived(ch, slot)
        total = part[ch, col].astype(jnp.float32)
        total = total + got[ch, 0].astype(jnp.float32) + got[ch, 1].astype(jnp.float32)

        @pl.when(at_end)
        def _():
            agg[:, lanes] = total.astype(agg.dtype)

        @pl.when(jnp.logical_not(at_end))
        def _():
            arrived(ch, 2)
            agg[:, lanes] = (total + got[ch, 2].astype(jnp.float32)).astype(agg.dtype)

    relay(0)
    for ch in range(n_chunk):
        if ch + AHEAD < n_chunk:
            send_own(ch + AHEAD)
        if ch + 1 < n_chunk:
            relay(ch + 1)
        for code in (1, 3, 5, 7):
            arrival(ch, code).wait_recv()
        own_copies[ch].wait()
        product = jnp.dot(
            dense[...],
            panel[ch].reshape(n_row * side, width),
            preferred_element_type=jnp.float32,
        )
        part[ch] = product.reshape(n_col, side, width).astype(part.dtype)
        send_parts(ch)
        if ch >= 1:
            pass_on(ch - 1)
    pass_on(n_chunk - 1)

    w_copy.wait()
    for ch in range(n_chunk - 1):
        finish(ch)
    early = (n_chunk - 1) * width
    for at in range(0, qkv.shape[1], 512):
        rows_early = jnp.dot(
            agg[:, :early], w_v[:early, at:at + 512], preferred_element_type=jnp.float32
        )
        rough[:, at:at + 512] = rows_early
    finish(n_chunk - 1)
    for at in range(0, qkv.shape[1], 512):
        rows_late = jnp.dot(
            agg[:, early:], w_v[early:, at:at + 512], preferred_element_type=jnp.float32
        )
        qkv[:, at:at + 512] = (rough[:, at:at + 512] + rows_late).astype(qkv.dtype)
    for ch in range(n_chunk):
        for sem in range(3):
            sum_copy(ch, part.at[ch, 0], 0, 2, sem).wait_send()
    for copy in sends:
        copy.wait_send()


def fused_body(n_row, n_col, features, adj_blocks, block_rows, block_cols, block_counts, w_qkv):
    cells, feat_width = features.shape[0], features.shape[2]
    slots, side = adj_blocks.shape[2], adj_blocks.shape[3]
    out_width = w_qkv.shape[1]
    n_chunk = feat_width // CHUNK
    vmem = pl.BlockSpec(memory_space=pltpu.VMEM)
    hbm = pl.BlockSpec(memory_space=pltpu.MemorySpace.HBM)
    dma = pltpu.SemaphoreType.DMA
    kind = features.dtype
    return pl.pallas_call(
        functools.partial(fused_kernel, n_col),
        out_shape=(
            jax.ShapeDtypeStruct((cells, feat_width), kind),
            jax.ShapeDtypeStruct((cells, out_width), kind),
        ),
        in_specs=[hbm, hbm, hbm, hbm, pl.BlockSpec(memory_space=pltpu.SMEM), hbm],
        out_specs=(vmem, vmem),
        scratch_shapes=[
            pltpu.VMEM((slots, side, side), kind),
            pltpu.VMEM((slots + 1, side, side), kind),
            pltpu.VMEM((n_col * side, n_row * side), kind),
            pltpu.VMEM((n_chunk, n_row, side, CHUNK), kind),
            pltpu.VMEM((n_chunk, n_col, side, CHUNK), kind),
            pltpu.VMEM((n_chunk, n_col, side, CHUNK), kind),
            pltpu.VMEM((n_chunk, side, CHUNK), kind),
            pltpu.VMEM((cells, out_width), jnp.float32),
            pltpu.VMEM(w_qkv.shape, kind),
            pltpu.VMEM((16, slots), jnp.int32),
            pltpu.VMEM((8, slots), jnp.int32),
            pltpu.SMEM((8, slots), jnp.int32),
            dma((5 + n_chunk,)),
            dma((n_chunk, 4)),
            dma((n_chunk, 8)),
            dma((n_chunk, 3)),
            dma((n_chunk, 3)),
            dma((n_chunk, n_col)),
        ],
        compiler_params=pltpu.CompilerParams(
            collective_id=0, has_side_effects=True, vmem_limit_bytes=56 << 20
        ),
    )(
        features[:, 0, :], adj_blocks[0, 0], block_rows[0], block_cols[0], block_counts, w_qkv
    )


def general_body(features, adj_blocks, block_rows, block_cols, block_counts, w_qkv):
    tile_blocks, row_ids, col_ids = adj_blocks[0, 0], block_rows[0, 0], block_cols[0, 0]
    side, feat_width = tile_blocks.shape[1], features.shape[2]
    slots = tile_blocks.shape[0]
    group = 32
    tile_cells = features.shape[0] * lax.axis_size("col")
    live = jnp.arange(slots, dtype=jnp.int32) < block_counts[0, 0]
    gathered = lax.all_gather(features, "row", axis=0, tiled=True)
    panel = gathered[:, 0, :].reshape(-1, side, feat_width)

    def one_group(partial_value, inputs):
        blocks_now, rows_now, cols_now, live_now = inputs
        products = jnp.einsum(
            "gij,gjf->gif", blocks_now, jnp.take(panel, cols_now, axis=0),
            preferred_element_type=jnp.float32,
        )
        products = jnp.where(live_now[:, None, None], products, jnp.float32(0.0))
        return partial_value.at[rows_now].add(products), None

    start = jnp.zeros((tile_cells // side, side, feat_width), jnp.float32)
    partial_value, _ = lax.scan(
        one_group, start,
        (
            tile_blocks.reshape(-1, group, side, side),
            row_ids.reshape(-1, group), col_ids.reshape(-1, group), live.reshape(-1, group),
        ),
    )
    summed = lax.psum_scatter(
        partial_value.reshape(tile_cells, feat_width).astype(jnp.bfloat16),
        "col", scatter_dimension=0, tiled=True,
    )
    qkv = jnp.dot(summed, w_qkv, preferred_element_type=jnp.float32).astype(jnp.bfloat16)
    return summed, qkv


def solution(mesh):
    n_row, n_col = mesh.shape["row"], mesh.shape["col"]
    body = functools.partial(fused_body, n_row, n_col) if n_row == 8 and n_col == 4 else general_body
    placed = (
        P("row", "col", None),
        P("row", "col", None, None, None),
        P("row", "col", None),
        P("row", "col", None),
        P("row", "col"),
        P(),
    )
    return jax.shard_map(
        body,
        mesh=mesh,
        in_specs=placed,
        out_specs=(P(("row", "col"), None), P(("row", "col"), None)),
        check_vma=False,
    )
```

```python
import functools

import jax
import jax.numpy as jnp
from jax import lax
from jax.experimental import pallas as pl
from jax.experimental.pallas import tpu as pltpu
from jax.sharding import PartitionSpec as P

MESH = pl.DeviceIdType.MESH
CHUNK = 128
UNROLL = 4
AHEAD = 2


def fused_kernel(
    n_col, feats, adj, rows, cols, count, agg,
    adj_v, prefix, dense, panel, part, got, joint, coords_v, meta_v, meta_s,
    local_sem, gather_send, gather_recv, relay_send, sum_send, sum_recv,
):
    slots, side = adj_v.shape[0], adj_v.shape[1]
    n_chunk, n_row = panel.shape[0], panel.shape[1]
    width = panel.shape[3]
    row, col = lax.axis_index("row"), lax.axis_index("col")
    chip_y, chip_x, core = row // 4, (row // 2) % 2, row % 2

    def partner(code):
        y = 1 - chip_y if code & 4 else chip_y
        x = 1 - chip_x if code & 2 else chip_x
        k = 1 - core if code & 1 else core
        return (y * 2 + x) * 2 + k

    coords_copies = [
        pltpu.make_async_copy(rows, coords_v.at[0:1], local_sem.at[3]),
        pltpu.make_async_copy(cols, coords_v.at[8:9], local_sem.at[4]),
    ]
    for copy in coords_copies:
        copy.start()
    adj_copy = pltpu.make_async_copy(adj, adj_v, local_sem.at[0])
    adj_copy.start()
    panel_own = [feats.at[:, pl.ds(ch * width, width)] for ch in range(n_chunk)]
    own_copies = [
        pltpu.make_async_copy(panel_own[ch], panel.at[ch, row], local_sem.at[5 + ch])
        for ch in range(n_chunk)
    ]
    for copy in own_copies:
        copy.start()

    barrier = pltpu.get_barrier_semaphore()
    for code in (1, 2, 4, 6):
        pl.semaphore_signal(barrier, inc=1, device_id={"row": partner(code)}, device_id_type=MESH)
    for step in range(1, n_col):
        pl.semaphore_signal(
            barrier, inc=1, device_id={"col": lax.rem(col + step, n_col)}, device_id_type=MESH
        )

    lane = lax.broadcasted_iota(jnp.int32, (slots, slots), 1)
    sub = lax.broadcasted_iota(jnp.int32, (slots, slots), 0)
    coords = n_col * n_row
    for copy in coords_copies:
        copy.wait()
    key = coords_v[0:1, :] * n_row + coords_v[8:9, :]
    key_lane = jnp.where(lane < count[0, 0], jnp.broadcast_to(key, (slots, slots)), coords)
    key_sub = jnp.transpose(key_lane)
    same_before = jnp.sum(
        ((key_lane == key_sub) & (lane < sub)).astype(jnp.int32), axis=1, keepdims=True
    )
    less = jnp.sum((key_lane < key_sub).astype(jnp.int32), axis=1, keepdims=True)
    placed = (less + same_before) == lane
    order = jnp.sum(jnp.where(placed, sub, 0), axis=0, keepdims=True)
    keep = jnp.sum(
        jnp.where(placed & (same_before > 0), 1, 0), axis=0, keepdims=True
    )
    upto = jnp.sum((key_sub <= lane).astype(jnp.int32), axis=0, keepdims=True)
    here = jnp.sum((key_sub == lane).astype(jnp.int32), axis=0, keepdims=True)
    last = jnp.where(here > 0, upto - 1, slots)
    meta_v[0:1, :] = order
    meta_v[1:2, :] = keep
    meta_v[2:3, :] = last
    meta_v[3:8, :] = jnp.zeros((5, slots), jnp.int32)
    meta_copy = pltpu.make_async_copy(meta_v, meta_s, local_sem.at[2])
    meta_copy.start()

    pl.semaphore_wait(barrier, 4 + n_col - 1)

    sends = []

    def send_own(ch):
        for slot, code in enumerate((6, 2, 4, 1)):
            copy = pltpu.make_async_remote_copy(
                src_ref=panel_own[ch],
                dst_ref=panel.at[ch, row],
                send_sem=gather_send.at[ch, slot],
                recv_sem=gather_recv.at[ch, code],
                device_id={"row": partner(code)},
                device_id_type=MESH,
            )
            copy.start()
            sends.append(copy)

    for ch in range(min(AHEAD, n_chunk)):
        send_own(ch)
    prefix[slots] = jnp.zeros((side, side), prefix.dtype)
    meta_copy.wait()
    adj_copy.wait()

    def add_slots(group, running):
        for inner in range(UNROLL):
            at = group * UNROLL + inner
            held = meta_s[1, at].astype(jnp.float32)
            running = running * held + adj_v[meta_s[0, at]].astype(jnp.float32)
            prefix[at] = running.astype(prefix.dtype)
        return running

    lax.fori_loop(0, slots // UNROLL, add_slots, jnp.zeros((side, side), jnp.float32))
    for block_row in range(n_col):
        for block_col in range(n_row):
            half = block_col % 2
            dense[
                block_col // 2,
                block_row * side:(block_row + 1) * side,
                half * side:(half + 1) * side,
            ] = prefix[meta_s[2, block_row * n_row + block_col]]

    def arrival(ch, code):
        return pltpu.make_async_remote_copy(
            src_ref=panel_own[ch],
            dst_ref=panel.at[ch, partner(code)],
            send_sem=gather_send.at[ch, 0],
            recv_sem=gather_recv.at[ch, code],
            device_id={"row": partner(1)},
            device_id_type=MESH,
        )

    def relay(ch):
        for slot, code in enumerate((2, 4, 6)):
            arrival(ch, code).wait_recv()
            copy = pltpu.make_async_remote_copy(
                src_ref=panel.at[ch, partner(code)],
                dst_ref=panel.at[ch, partner(code)],
                send_sem=relay_send.at[ch, slot],
                recv_sem=gather_recv.at[ch, code + 1],
                device_id={"row": partner(1)},
                device_id_type=MESH,
            )
            copy.start()
            sends.append(copy)

    at_end = (col == 0) | (col == n_col - 1)
    upper = col // 2

    def along(place):
        return place + upper * (n_col - 1 - 2 * place)

    def sum_copy(ch, source, slot, place, sem):
        return pltpu.make_async_remote_copy(
            src_ref=source,
            dst_ref=got.at[ch, slot],
            send_sem=sum_send.at[ch, sem],
            recv_sem=sum_recv.at[ch, slot],
            device_id={"col": along(place)},
            device_id_type=MESH,
        )

    def arrived(ch, slot):
        sum_copy(ch, part.at[ch, 0], slot, 2, 0).wait_recv()

    def send_parts(ch):
        @pl.when(at_end)
        def _():
            sum_copy(ch, part.at[ch, along(3)], 3, 1, 0).start()
            sum_copy(ch, part.at[ch, along(2)], 2, 2, 1).start()
            sum_copy(ch, part.at[ch, along(1)], 0, 1, 2).start()

        @pl.when(jnp.logical_not(at_end))
        def _():
            sum_copy(ch, part.at[ch, along(2)], 1, 2, 1).start()
            sum_copy(ch, part.at[ch, along(0)], 0, 0, 2).start()

    def pass_on(ch):
        @pl.when(jnp.logical_not(at_end))
        def _():
            arrived(ch, 3)
            both = part[ch, along(3)].astype(jnp.float32) + got[ch, 3].astype(jnp.float32)
            joint[ch] = both.astype(joint.dtype)
            sum_copy(ch, joint.at[ch], 1, 3, 0).start()

    def finish(ch):
        lanes = slice(ch * width, (ch + 1) * width)
        for slot in (0, 1):
            arrived(ch, slot)
        total = part[ch, col].astype(jnp.float32)
        total = total + got[ch, 0].astype(jnp.float32) + got[ch, 1].astype(jnp.float32)

        @pl.when(at_end)
        def _():
            agg[:, lanes] = total.astype(agg.dtype)

        @pl.when(jnp.logical_not(at_end))
        def _():
            arrived(ch, 2)
            agg[:, lanes] = (total + got[ch, 2].astype(jnp.float32)).astype(agg.dtype)

    relay(0)
    for ch in range(n_chunk):
        if ch + AHEAD < n_chunk:
            send_own(ch + AHEAD)
        product = None
        for code in (0, 2, 4, 6):
            if code == 0:
                own_copies[ch].wait()
            arrival(ch, code + 1).wait_recv()
            pair = partner(code) // 2
            piece = jnp.dot(
                dense[pair],
                panel[ch, pl.ds(pair * 2, 2)].reshape(2 * side, width),
                preferred_element_type=jnp.float32,
            )
            product = piece if product is None else product + piece
        part[ch] = product.reshape(n_col, side, width).astype(part.dtype)
        send_parts(ch)
        if ch + 1 < n_chunk:
            relay(ch + 1)
        if ch >= 1:
            pass_on(ch - 1)
    pass_on(n_chunk - 1)

    for ch in range(n_chunk):
        finish(ch)
    for ch in range(n_chunk):
        for sem in range(3):
            sum_copy(ch, part.at[ch, 0], 0, 2, sem).wait_send()
    for copy in sends:
        copy.wait_send()


def project_kernel(agg, w, agg_out, qkv, agg_v, w_v, qkv_v, in_sem, out_sem):
    width = w.shape[1]
    step = 512 if width % 512 == 0 else width
    agg_copy = pltpu.make_async_copy(agg, agg_v, in_sem.at[0])
    agg_copy.start()
    w_copies = []
    for at in range(0, width, step):
        copy = pltpu.make_async_copy(
            w.at[:, pl.ds(at, step)], w_v.at[:, pl.ds(at, step)], in_sem.at[1 + at // step]
        )
        copy.start()
        w_copies.append(copy)
    agg_copy.wait()
    outs = [pltpu.make_async_copy(agg_v, agg_out, out_sem.at[0])]
    outs[0].start()
    for at, w_copy in zip(range(0, width, step), w_copies):
        w_copy.wait()
        lanes = slice(at, at + step)
        qkv_v[:, lanes] = jnp.dot(
            agg_v[...], w_v[:, lanes], preferred_element_type=jnp.float32
        ).astype(qkv_v.dtype)
        copy = pltpu.make_async_copy(
            qkv_v.at[:, pl.ds(at, step)], qkv.at[:, pl.ds(at, step)], out_sem.at[1 + at // step]
        )
        copy.start()
        outs.append(copy)
    for copy in outs:
        copy.wait()


def fused_body(n_row, n_col, features, adj_blocks, block_rows, block_cols, block_counts, w_qkv):
    cells, feat_width = features.shape[0], features.shape[2]
    slots, side = adj_blocks.shape[2], adj_blocks.shape[3]
    out_width = w_qkv.shape[1]
    n_chunk = feat_width // CHUNK
    vmem = pl.BlockSpec(memory_space=pltpu.VMEM)
    hbm = pl.BlockSpec(memory_space=pltpu.MemorySpace.HBM)
    dma = pltpu.SemaphoreType.DMA
    kind = features.dtype
    summed = pl.pallas_call(
        functools.partial(fused_kernel, n_col),
        out_shape=jax.ShapeDtypeStruct((cells, feat_width), kind),
        in_specs=[hbm, hbm, hbm, hbm, pl.BlockSpec(memory_space=pltpu.SMEM)],
        out_specs=vmem,
        scratch_shapes=[
            pltpu.VMEM((slots, side, side), kind),
            pltpu.VMEM((slots + 1, side, side), kind),
            pltpu.VMEM((n_row // 2, n_col * side, 2 * side), kind),
            pltpu.VMEM((n_chunk, n_row, side, CHUNK), kind),
            pltpu.VMEM((n_chunk, n_col, side, CHUNK), kind),
            pltpu.VMEM((n_chunk, n_col, side, CHUNK), kind),
            pltpu.VMEM((n_chunk, side, CHUNK), kind),
            pltpu.VMEM((16, slots), jnp.int32),
            pltpu.VMEM((8, slots), jnp.int32),
            pltpu.SMEM((8, slots), jnp.int32),
            dma((5 + n_chunk,)),
            dma((n_chunk, 4)),
            dma((n_chunk, 8)),
            dma((n_chunk, 3)),
            dma((n_chunk, 3)),
            dma((n_chunk, n_col)),
        ],
        compiler_params=pltpu.CompilerParams(
            collective_id=0, has_side_effects=True, vmem_limit_bytes=56 << 20
        ),
    )(features[:, 0, :], adj_blocks[0, 0], block_rows[0], block_cols[0], block_counts)
    return pl.pallas_call(
        project_kernel,
        out_shape=(
            jax.ShapeDtypeStruct((cells, feat_width), kind),
            jax.ShapeDtypeStruct((cells, out_width), kind),
        ),
        in_specs=[hbm, hbm],
        out_specs=(hbm, hbm),
        scratch_shapes=[
            pltpu.VMEM((cells, feat_width), kind),
            pltpu.VMEM(w_qkv.shape, kind),
            pltpu.VMEM((cells, out_width), kind),
            dma((1 + max(1, out_width // 512),)),
            dma((1 + max(1, out_width // 512),)),
        ],
        compiler_params=pltpu.CompilerParams(vmem_limit_bytes=56 << 20),
    )(summed, w_qkv)


def general_body(features, adj_blocks, block_rows, block_cols, block_counts, w_qkv):
    tile_blocks, row_ids, col_ids = adj_blocks[0, 0], block_rows[0, 0], block_cols[0, 0]
    side, feat_width = tile_blocks.shape[1], features.shape[2]
    slots = tile_blocks.shape[0]
    group = 32
    tile_cells = features.shape[0] * lax.axis_size("col")
    live = jnp.arange(slots, dtype=jnp.int32) < block_counts[0, 0]
    gathered = lax.all_gather(features, "row", axis=0, tiled=True)
    panel = gathered[:, 0, :].reshape(-1, side, feat_width)

    def one_group(partial_value, inputs):
        blocks_now, rows_now, cols_now, live_now = inputs
        products = jnp.einsum(
            "gij,gjf->gif", blocks_now, jnp.take(panel, cols_now, axis=0),
            preferred_element_type=jnp.float32,
        )
        products = jnp.where(live_now[:, None, None], products, jnp.float32(0.0))
        return partial_value.at[rows_now].add(products), None

    start = jnp.zeros((tile_cells // side, side, feat_width), jnp.float32)
    partial_value, _ = lax.scan(
        one_group, start,
        (
            tile_blocks.reshape(-1, group, side, side),
            row_ids.reshape(-1, group), col_ids.reshape(-1, group), live.reshape(-1, group),
        ),
    )
    summed = lax.psum_scatter(
        partial_value.reshape(tile_cells, feat_width).astype(jnp.bfloat16),
        "col", scatter_dimension=0, tiled=True,
    )
    qkv = jnp.dot(summed, w_qkv, preferred_element_type=jnp.float32).astype(jnp.bfloat16)
    return summed, qkv


def solution(mesh):
    n_row, n_col = mesh.shape["row"], mesh.shape["col"]
    body = functools.partial(fused_body, n_row, n_col) if n_row == 8 and n_col == 4 else general_body
    placed = (
        P("row", "col", None),
        P("row", "col", None, None, None),
        P("row", "col", None),
        P("row", "col", None),
        P("row", "col"),
        P(),
    )
    return jax.shard_map(
        body,
        mesh=mesh,
        in_specs=placed,
        out_specs=(P(("row", "col"), None), P(("row", "col"), None)),
        check_vma=False,
    )
```

```python
import functools

import jax
import jax.numpy as jnp
from jax import lax
from jax.experimental import pallas as pl
from jax.experimental.pallas import tpu as pltpu
from jax.sharding import PartitionSpec as P

MESH = pl.DeviceIdType.MESH
CHUNK = 128
UNROLL = 8
AHEAD = 2


def fused_kernel(
    n_col, feats, adj, rows, cols, count, agg,
    adj_v, prefix, dense, panel, part, got, joint, coords_v, meta_v, meta_s,
    local_sem, gather_send, gather_recv, relay_send, sum_send, sum_recv,
):
    slots, side = adj_v.shape[0], adj_v.shape[1]
    n_chunk, n_row = panel.shape[0], panel.shape[1]
    width = panel.shape[3]
    row, col = lax.axis_index("row"), lax.axis_index("col")
    chip_y, chip_x, core = row // 4, (row // 2) % 2, row % 2

    def partner(code):
        y = 1 - chip_y if code & 4 else chip_y
        x = 1 - chip_x if code & 2 else chip_x
        k = 1 - core if code & 1 else core
        return (y * 2 + x) * 2 + k

    coords_copies = [
        pltpu.make_async_copy(rows, coords_v.at[0:1], local_sem.at[3]),
        pltpu.make_async_copy(cols, coords_v.at[8:9], local_sem.at[4]),
    ]
    for copy in coords_copies:
        copy.start()
    adj_copy = pltpu.make_async_copy(adj, adj_v, local_sem.at[0])
    adj_copy.start()
    panel_own = [feats.at[:, pl.ds(ch * width, width)] for ch in range(n_chunk)]
    own_copies = [
        pltpu.make_async_copy(panel_own[ch], panel.at[ch, row], local_sem.at[5 + ch])
        for ch in range(n_chunk)
    ]
    for copy in own_copies:
        copy.start()

    barrier = pltpu.get_barrier_semaphore()
    for code in (1, 2, 4, 6):
        pl.semaphore_signal(barrier, inc=1, device_id={"row": partner(code)}, device_id_type=MESH)
    for step in range(1, n_col):
        pl.semaphore_signal(
            barrier, inc=1, device_id={"col": lax.rem(col + step, n_col)}, device_id_type=MESH
        )

    pl.semaphore_wait(barrier, 4 + n_col - 1)

    sends = []

    def send_own(ch):
        for slot, code in enumerate((6, 2, 4, 1)):
            copy = pltpu.make_async_remote_copy(
                src_ref=panel_own[ch],
                dst_ref=panel.at[ch, row],
                send_sem=gather_send.at[ch, slot],
                recv_sem=gather_recv.at[ch, code],
                device_id={"row": partner(code)},
                device_id_type=MESH,
            )
            copy.start()
            sends.append(copy)

    for ch in range(min(AHEAD, n_chunk)):
        send_own(ch)
    lane = lax.broadcasted_iota(jnp.int32, (slots, slots), 1)
    sub = lax.broadcasted_iota(jnp.int32, (slots, slots), 0)
    coords = n_col * n_row
    for copy in coords_copies:
        copy.wait()
    key = coords_v[0:1, :] * n_row + coords_v[8:9, :]
    key_lane = jnp.where(lane < count[0, 0], jnp.broadcast_to(key, (slots, slots)), coords)
    key_sub = jnp.transpose(key_lane)
    same_before = jnp.sum(
        ((key_lane == key_sub) & (lane < sub)).astype(jnp.int32), axis=1, keepdims=True
    )
    less = jnp.sum((key_lane < key_sub).astype(jnp.int32), axis=1, keepdims=True)
    placed = (less + same_before) == lane
    order = jnp.sum(jnp.where(placed, sub, 0), axis=0, keepdims=True)
    keep = jnp.sum(
        jnp.where(placed & (same_before > 0), 1, 0), axis=0, keepdims=True
    )
    upto = jnp.sum((key_sub <= lane).astype(jnp.int32), axis=0, keepdims=True)
    here = jnp.sum((key_sub == lane).astype(jnp.int32), axis=0, keepdims=True)
    last = jnp.where(here > 0, upto - 1, slots)
    meta_v[0:1, :] = order
    meta_v[1:2, :] = keep
    meta_v[2:3, :] = last
    meta_v[3:8, :] = jnp.zeros((5, slots), jnp.int32)
    meta_copy = pltpu.make_async_copy(meta_v, meta_s, local_sem.at[2])
    meta_copy.start()

    prefix[slots] = jnp.zeros((side, side), prefix.dtype)
    meta_copy.wait()
    adj_copy.wait()

    def add_slots(group, running):
        for inner in range(UNROLL):
            at = group * UNROLL + inner
            held = meta_s[1, at].astype(jnp.float32)
            running = running * held + adj_v[meta_s[0, at]].astype(jnp.float32)
            prefix[at] = running.astype(prefix.dtype)
        return running

    lax.fori_loop(0, slots // UNROLL, add_slots, jnp.zeros((side, side), jnp.float32))
    for block_row in range(n_col):
        for block_col in range(n_row):
            half = block_col % 2
            dense[
                block_col // 2,
                block_row * side:(block_row + 1) * side,
                half * side:(half + 1) * side,
            ] = prefix[meta_s[2, block_row * n_row + block_col]]

    def arrival(ch, code):
        return pltpu.make_async_remote_copy(
            src_ref=panel_own[ch],
            dst_ref=panel.at[ch, partner(code)],
            send_sem=gather_send.at[ch, 0],
            recv_sem=gather_recv.at[ch, code],
            device_id={"row": partner(1)},
            device_id_type=MESH,
        )

    def relay(ch):
        for slot, code in enumerate((2, 4, 6)):
            arrival(ch, code).wait_recv()
            copy = pltpu.make_async_remote_copy(
                src_ref=panel.at[ch, partner(code)],
                dst_ref=panel.at[ch, partner(code)],
                send_sem=relay_send.at[ch, slot],
                recv_sem=gather_recv.at[ch, code + 1],
                device_id={"row": partner(1)},
                device_id_type=MESH,
            )
            copy.start()
            sends.append(copy)

    at_end = (col == 0) | (col == n_col - 1)
    upper = col // 2

    def along(place):
        return place + upper * (n_col - 1 - 2 * place)

    def sum_copy(ch, source, slot, place, sem):
        return pltpu.make_async_remote_copy(
            src_ref=source,
            dst_ref=got.at[ch, slot],
            send_sem=sum_send.at[ch, sem],
            recv_sem=sum_recv.at[ch, slot],
            device_id={"col": along(place)},
            device_id_type=MESH,
        )

    def arrived(ch, slot):
        sum_copy(ch, part.at[ch, 0], slot, 2, 0).wait_recv()

    def send_parts(ch):
        @pl.when(at_end)
        def _():
            if ch == n_chunk - 1:
                sum_copy(ch, part.at[ch, along(3)], 1, 3, 0).start()
            else:
                sum_copy(ch, part.at[ch, along(3)], 3, 1, 0).start()
            sum_copy(ch, part.at[ch, along(2)], 2, 2, 1).start()
            sum_copy(ch, part.at[ch, along(1)], 0, 1, 2).start()

        @pl.when(jnp.logical_not(at_end))
        def _():
            if ch == n_chunk - 1:
                sum_copy(ch, part.at[ch, along(3)], 3, 3, 0).start()
            sum_copy(ch, part.at[ch, along(2)], 1, 2, 1).start()
            sum_copy(ch, part.at[ch, along(0)], 0, 0, 2).start()

    def pass_on(ch):
        @pl.when(jnp.logical_not(at_end))
        def _():
            arrived(ch, 3)
            both = part[ch, along(3)].astype(jnp.float32) + got[ch, 3].astype(jnp.float32)
            joint[ch] = both.astype(joint.dtype)
            sum_copy(ch, joint.at[ch], 1, 3, 0).start()

    def finish(ch):
        lanes = slice(ch * width, (ch + 1) * width)
        for slot in (0, 1):
            arrived(ch, slot)
        total = part[ch, col].astype(jnp.float32)
        total = total + got[ch, 0].astype(jnp.float32) + got[ch, 1].astype(jnp.float32)

        @pl.when(at_end)
        def _():
            if ch == n_chunk - 1:
                arrived(ch, 3)
                agg[:, lanes] = (total + got[ch, 3].astype(jnp.float32)).astype(agg.dtype)
            else:
                agg[:, lanes] = total.astype(agg.dtype)

        @pl.when(jnp.logical_not(at_end))
        def _():
            arrived(ch, 2)
            agg[:, lanes] = (total + got[ch, 2].astype(jnp.float32)).astype(agg.dtype)

    relay(0)
    for ch in range(n_chunk):
        if ch + AHEAD < n_chunk:
            send_own(ch + AHEAD)
        product = None
        for code in (0, 2, 4, 6):
            if code == 0:
                own_copies[ch].wait()
            arrival(ch, code + 1).wait_recv()
            pair = partner(code) // 2
            piece = jnp.dot(
                dense[pair],
                panel[ch, pl.ds(pair * 2, 2)].reshape(2 * side, width),
                preferred_element_type=jnp.float32,
            )
            product = piece if product is None else product + piece
        part[ch] = product.reshape(n_col, side, width).astype(part.dtype)
        send_parts(ch)
        if ch >= 1:
            pass_on(ch - 1)
        if ch + 1 < n_chunk:
            relay(ch + 1)

    for ch in range(n_chunk):
        finish(ch)
    for ch in range(n_chunk):
        for sem in range(3):
            sum_copy(ch, part.at[ch, 0], 0, 2, sem).wait_send()
    for copy in sends:
        copy.wait_send()


def project_kernel(agg, w, agg_out, qkv, agg_v, w_v, qkv_v, in_sem, out_sem):
    width = w.shape[1]
    step = 512 if width % 512 == 0 else width
    agg_copy = pltpu.make_async_copy(agg, agg_v, in_sem.at[0])
    agg_copy.start()
    w_copies = []
    for at in range(0, width, step):
        copy = pltpu.make_async_copy(
            w.at[:, pl.ds(at, step)], w_v.at[:, pl.ds(at, step)], in_sem.at[1 + at // step]
        )
        copy.start()
        w_copies.append(copy)
    agg_copy.wait()
    outs = [pltpu.make_async_copy(agg_v, agg_out, out_sem.at[0])]
    outs[0].start()
    for at, w_copy in zip(range(0, width, step), w_copies):
        w_copy.wait()
        lanes = slice(at, at + step)
        qkv_v[:, lanes] = jnp.dot(
            agg_v[...], w_v[:, lanes], preferred_element_type=jnp.float32
        ).astype(qkv_v.dtype)
        copy = pltpu.make_async_copy(
            qkv_v.at[:, pl.ds(at, step)], qkv.at[:, pl.ds(at, step)], out_sem.at[1 + at // step]
        )
        copy.start()
        outs.append(copy)
    for copy in outs:
        copy.wait()


def fused_body(n_row, n_col, features, adj_blocks, block_rows, block_cols, block_counts, w_qkv):
    cells, feat_width = features.shape[0], features.shape[2]
    slots, side = adj_blocks.shape[2], adj_blocks.shape[3]
    out_width = w_qkv.shape[1]
    n_chunk = feat_width // CHUNK
    vmem = pl.BlockSpec(memory_space=pltpu.VMEM)
    hbm = pl.BlockSpec(memory_space=pltpu.MemorySpace.HBM)
    dma = pltpu.SemaphoreType.DMA
    kind = features.dtype
    summed = pl.pallas_call(
        functools.partial(fused_kernel, n_col),
        out_shape=jax.ShapeDtypeStruct((cells, feat_width), kind),
        in_specs=[hbm, hbm, hbm, hbm, pl.BlockSpec(memory_space=pltpu.SMEM)],
        out_specs=vmem,
        scratch_shapes=[
            pltpu.VMEM((slots, side, side), kind),
            pltpu.VMEM((slots + 1, side, side), kind),
            pltpu.VMEM((n_row // 2, n_col * side, 2 * side), kind),
            pltpu.VMEM((n_chunk, n_row, side, CHUNK), kind),
            pltpu.VMEM((n_chunk, n_col, side, CHUNK), kind),
            pltpu.VMEM((n_chunk, n_col, side, CHUNK), kind),
            pltpu.VMEM((n_chunk, side, CHUNK), kind),
            pltpu.VMEM((16, slots), jnp.int32),
            pltpu.VMEM((8, slots), jnp.int32),
            pltpu.SMEM((8, slots), jnp.int32),
            dma((5 + n_chunk,)),
            dma((n_chunk, 4)),
            dma((n_chunk, 8)),
            dma((n_chunk, 3)),
            dma((n_chunk, 3)),
            dma((n_chunk, n_col)),
        ],
        compiler_params=pltpu.CompilerParams(
            collective_id=0, has_side_effects=True, vmem_limit_bytes=56 << 20
        ),
    )(features[:, 0, :], adj_blocks[0, 0], block_rows[0], block_cols[0], block_counts)
    return pl.pallas_call(
        project_kernel,
        out_shape=(
            jax.ShapeDtypeStruct((cells, feat_width), kind),
            jax.ShapeDtypeStruct((cells, out_width), kind),
        ),
        in_specs=[hbm, hbm],
        out_specs=(hbm, hbm),
        scratch_shapes=[
            pltpu.VMEM((cells, feat_width), kind),
            pltpu.VMEM(w_qkv.shape, kind),
            pltpu.VMEM((cells, out_width), kind),
            dma((1 + max(1, out_width // 512),)),
            dma((1 + max(1, out_width // 512),)),
        ],
        compiler_params=pltpu.CompilerParams(vmem_limit_bytes=56 << 20),
    )(summed, w_qkv)


def general_body(features, adj_blocks, block_rows, block_cols, block_counts, w_qkv):
    tile_blocks, row_ids, col_ids = adj_blocks[0, 0], block_rows[0, 0], block_cols[0, 0]
    side, feat_width = tile_blocks.shape[1], features.shape[2]
    slots = tile_blocks.shape[0]
    group = 32
    tile_cells = features.shape[0] * lax.axis_size("col")
    live = jnp.arange(slots, dtype=jnp.int32) < block_counts[0, 0]
    gathered = lax.all_gather(features, "row", axis=0, tiled=True)
    panel = gathered[:, 0, :].reshape(-1, side, feat_width)

    def one_group(partial_value, inputs):
        blocks_now, rows_now, cols_now, live_now = inputs
        products = jnp.einsum(
            "gij,gjf->gif", blocks_now, jnp.take(panel, cols_now, axis=0),
            preferred_element_type=jnp.float32,
        )
        products = jnp.where(live_now[:, None, None], products, jnp.float32(0.0))
        return partial_value.at[rows_now].add(products), None

    start = jnp.zeros((tile_cells // side, side, feat_width), jnp.float32)
    partial_value, _ = lax.scan(
        one_group, start,
        (
            tile_blocks.reshape(-1, group, side, side),
            row_ids.reshape(-1, group), col_ids.reshape(-1, group), live.reshape(-1, group),
        ),
    )
    summed = lax.psum_scatter(
        partial_value.reshape(tile_cells, feat_width).astype(jnp.bfloat16),
        "col", scatter_dimension=0, tiled=True,
    )
    qkv = jnp.dot(summed, w_qkv, preferred_element_type=jnp.float32).astype(jnp.bfloat16)
    return summed, qkv


def solution(mesh):
    n_row, n_col = mesh.shape["row"], mesh.shape["col"]
    body = functools.partial(fused_body, n_row, n_col) if n_row == 8 and n_col == 4 else general_body
    placed = (
        P("row", "col", None),
        P("row", "col", None, None, None),
        P("row", "col", None),
        P("row", "col", None),
        P("row", "col"),
        P(),
    )
    return jax.shard_map(
        body,
        mesh=mesh,
        in_specs=placed,
        out_specs=(P(("row", "col"), None), P(("row", "col"), None)),
        check_vma=False,
    )
```
